1024 devices in a mesh: span: 8 (over x, core), seq: 32 (over z), mp: 4 (over y).
Axes of the slice: x: 4, y: 4, z: 32, core: 2. Of those that a mesh axis runs over, the one named last changes fastest.
Arguments:
- queries: bfloat16 [8, 2048, 3072], P('span', 'seq', 'mp'), may hold values from -256 to 256
- keys_values: bfloat16 [2, 8, 2048, 512], P(None, 'span', 'seq', 'mp'), may hold values from -200 to 200
- clip_tokens: int32 [8], replicated, may hold values from 512 to 2048, as said below
- noise_level: int32 [8], replicated, may hold values from 0 to 63
- level_gate: bfloat16 [64, 3072], P(None, 'mp'), may hold values from -3 to 3
- out_gain: bfloat16 [3072], P('mp'), may hold values from 0.099609375 to 1.8984375
Outputs:
- layer_out: bfloat16 [8, 2048, 3072], P('span', 'seq', 'mp')
The draws below stay inside these ranges and needn't reach their ends.
Inputs may be any that keep to these rules, and one draw needn't show every extreme that they name: `clip_tokens`: each clip's live slots are its first ones; some clip fills all 2048 slots.
All inputs are finite; a program needn't handle non-finite values.
Results may differ from the reference program's by a relative error of at most 0.0065.
Values may be sent and summed in bfloat16 or wider, within the bound.
A program may use at most 32 MiB of HBM per device.

```python
import math
import jax
import jax.numpy as jnp
from jax import lax

HEADS = 24
KVH = 4
HD = 128
LEVELS = 64
TOK_DEV = 64
CLIPS = 8
SLOTS = 2048


def shared_tokens(base_key):
    root = jax.random.fold_in(base_key, 11)
    key_one = jax.random.fold_in(root, 1)
    key_two = jax.random.fold_in(root, 2)
    key_three = jax.random.fold_in(root, 3)
    full_shape = (CLIPS, SLOTS, KVH, HD)
    key_rows = jnp.clip(jax.random.normal(key_one, full_shape, jnp.float32), -4.0, 4.0)
    head_top = 3.0
    head_scale = head_top ** (jnp.arange(KVH, dtype=jnp.float32) / max(KVH - 1, 1))
    row_scale = 0.5 * jnp.exp(jax.random.uniform(key_three, (CLIPS, SLOTS, 1, 1), jnp.float32, 0.0, math.log(10.0)))
    value_rows = jnp.clip(jax.random.normal(key_two, full_shape, jnp.float32), -4.0, 4.0) * head_scale[:, None] * row_scale
    return (key_rows, value_rows)


def draw_keys_values(key, part):
    key_rows, value_rows = shared_tokens(key)
    stacked = jnp.stack([key_rows.reshape(CLIPS, SLOTS, KVH * HD), value_rows.reshape(CLIPS, SLOTS, KVH * HD)])
    return stacked.astype(jnp.bfloat16)


def draw_queries(key, part):
    query_key = jax.random.fold_in(key, 23)
    full_shape = (CLIPS, SLOTS, HEADS, HD)
    query_rows = jnp.clip(2.0 * jax.random.normal(query_key, full_shape, jnp.float32), -12.0, 12.0)
    return query_rows.reshape(CLIPS, SLOTS, HEADS * HD).astype(jnp.bfloat16)


def draw_clip_tokens(key, part):
    root = jax.random.fold_in(key, 37)
    lengths = jax.random.randint(jax.random.fold_in(root, 1), (CLIPS,), SLOTS // 4, SLOTS + 1)
    filled = jax.random.randint(jax.random.fold_in(root, 2), (), 0, CLIPS)
    lengths = jnp.where(jnp.arange(CLIPS) == filled, SLOTS, lengths)
    return lengths.astype(jnp.int32)


def place_ends(array, stream_key, low, top_value):
    spot = [jax.random.randint(jax.random.fold_in(stream_key, axis), (), 0, length) for axis, length in enumerate(array.shape)]
    main_axis = array.shape.index(max(array.shape))
    next_to = spot[:main_axis] + [(spot[main_axis] + 1) % array.shape[main_axis]] + spot[main_axis + 1:]
    return array.at[tuple(spot)].set(low).at[tuple(next_to)].set(top_value)


def levels(stream_key, extent, pieces, smallest, largest):
    def one(position, shards_of):
        heights = jax.random.uniform(jax.random.fold_in(jax.random.fold_in(stream_key, 6), position), (shards_of,), jnp.float32, smallest / len(pieces), largest / len(pieces))
        return jnp.repeat(jnp.exp(heights), extent[position] // shards_of).reshape((-1,) + (1,) * (len(extent) - position - 1))

    factor_of = one(*pieces[0])
    for cut in pieces[1:]:
        factor_of = factor_of * one(*cut)
    return factor_of


def centred(stream_key, shape, spread, limit, split=(), kind=jnp.bfloat16):
    gain = levels(stream_key, shape, split, -0.22, 0.18) if split else 1.0
    drawn = jax.random.normal(stream_key, shape, jnp.float32) * spread * gain
    return jnp.minimum(jnp.maximum(drawn, -limit), limit).astype(kind)


def setup_inputs(seed: int = 0) -> dict:
    seeds = jax.random.split(jax.random.key(seed), 7)
    queries = draw_queries(jax.random.fold_in(seeds[6], 71), 0)
    keys_values = draw_keys_values(jax.random.fold_in(seeds[6], 71), 0)
    clip_tokens = draw_clip_tokens(jax.random.fold_in(seeds[6], 71), 0)
    noise_level = place_ends(jax.random.randint(seeds[3], (CLIPS,), 0, LEVELS), jax.random.fold_in(seeds[3], 1), 0, LEVELS - 1).astype(jnp.int32)
    level_gate = centred(seeds[4], (LEVELS, HEADS * HD), 0.5, 3.0, ((1, 4),))
    out_gain = jnp.clip(1.0 + 0.18 * jax.random.normal(seeds[5], (HEADS * HD,), jnp.float32), 0.099609375, 1.8984375).astype(jnp.bfloat16)
    return {"queries": queries, "keys_values": keys_values, "clip_tokens": clip_tokens, "noise_level": noise_level, "level_gate": level_gate, "out_gain": out_gain}


def reference(queries, keys_values, clip_tokens, noise_level, level_gate, out_gain):
    clip_count, slot_count, width = queries.shape
    group_size = HEADS // KVH
    score_scale = 1.0 / math.sqrt(HD)
    key_rows = keys_values[0].astype(jnp.float32).reshape(clip_count * slot_count, KVH, HD)
    value_rows = keys_values[1].astype(jnp.float32).reshape(clip_count * slot_count, KVH, HD)
    positions = jnp.arange(clip_count * slot_count, dtype=jnp.int32)
    holder = positions // slot_count
    slot_index = positions - holder * slot_count
    key_usable = slot_index < clip_tokens[holder]
    block_count = clip_count * slot_count // TOK_DEV
    blocks = queries.reshape(block_count, TOK_DEV, KVH, group_size, HD)

    def one_block(block_index):
        query_rows = lax.dynamic_index_in_dim(blocks, block_index, 0, keepdims=False).astype(jnp.float32)
        own_clip = block_index * TOK_DEV // slot_count
        allowed = key_usable & (holder <= own_clip)
        scores = jnp.einsum('tgrd,kgd->tgrk', query_rows, key_rows) * score_scale
        scores = jnp.where(allowed, scores, -jnp.inf)
        row_max = lax.optimization_barrier(jnp.max(scores, axis=-1, keepdims=True))
        weights = jnp.exp(scores - row_max)
        weight_sum = lax.optimization_barrier(jnp.sum(weights, axis=-1))
        rounded = lax.optimization_barrier(weights.astype(jnp.bfloat16)).astype(jnp.float32)
        mixed = jnp.einsum('tgrk,kgd->tgrd', rounded, value_rows)
        return (mixed / weight_sum[..., None]).reshape(TOK_DEV, width)
    attended = lax.map(one_block, jnp.arange(block_count, dtype=jnp.int32)).reshape(clip_count, slot_count, width)
    mean_square = lax.optimization_barrier(jnp.mean(attended * attended, axis=-1, keepdims=True))
    gate_rows = level_gate[noise_level].astype(jnp.float32)
    normed = attended * lax.rsqrt(mean_square + 1e-06) * out_gain.astype(jnp.float32) * (1.0 + gate_rows[:, None, :])
    usable = jnp.arange(slot_count, dtype=jnp.int32)[None, :] < clip_tokens[:, None]
    return jnp.where(usable[..., None], normed, 0.0).astype(jnp.bfloat16)
```

```python
import functools
import math

import jax
import jax.numpy as jnp
from jax import lax
from jax.experimental import pallas as pl
from jax.experimental.pallas import tpu as pltpu
from jax.sharding import PartitionSpec as P

HEADS = 24
KVH = 4
HD = 128
GROUP = HEADS // KVH
TOK = 64
NX = 4
NZ = 32
NY = 4
ROWS = GROUP * TOK
EXP_SCALE = math.log2(math.e) / math.sqrt(HD)
LOW = -1e30
MESH = pl.DeviceIdType.MESH


def kernel(
    tok_ref, noise_ref, q_ref, kv_ref, gate_ref, gain_ref, out_ref,
    kvbuf, vtbuf, qbuf, acc, stat, obuf, sbuf, orecv, srecv, sqsend, sqrecv,
    z_send, z_recv, c_send, c_recv, q_send, q_recv, o_send, o_recv, s_send, s_recv, y_send, y_recv,
):
    span = lax.axis_index("span")
    z = lax.axis_index("seq")
    y = lax.axis_index("mp")
    x = span // 2
    core = span % 2
    sibling = span + 1 - 2 * core

    def along_z(step):
        return {"seq": (z + step + NZ) % NZ}

    def z_copy(src, dst_slot, step):
        return pltpu.make_async_remote_copy(
            src_ref=src, dst_ref=kvbuf.at[0, dst_slot],
            send_sem=z_send.at[dst_slot], recv_sem=z_recv.at[dst_slot],
            device_id=along_z(step), device_id_type=MESH,
        )

    def c_copy(src, slot):
        return pltpu.make_async_remote_copy(
            src_ref=src, dst_ref=kvbuf.at[1, slot],
            send_sem=c_send.at[slot], recv_sem=c_recv.at[slot],
            device_id={"span": sibling}, device_id_type=MESH,
        )

    def q_copy(d):
        return pltpu.make_async_remote_copy(
            src_ref=q_ref, dst_ref=qbuf.at[d],
            send_sem=q_send.at[d], recv_sem=q_recv.at[d],
            device_id={"span": (span - 2 * d + 8) % 8}, device_id_type=MESH,
        )

    def o_copy(d):
        return pltpu.make_async_remote_copy(
            src_ref=obuf.at[d], dst_ref=orecv.at[d],
            send_sem=o_send.at[d], recv_sem=o_recv.at[d],
            device_id={"span": (span + 2 * d) % 8}, device_id_type=MESH,
        )

    def s_copy(d):
        return pltpu.make_async_remote_copy(
            src_ref=sbuf.at[d], dst_ref=srecv.at[d],
            send_sem=s_send.at[d], recv_sem=s_recv.at[d],
            device_id={"span": (span + 2 * d) % 8}, device_id_type=MESH,
        )

    def y_copy(d):
        return pltpu.make_async_remote_copy(
            src_ref=sqsend, dst_ref=sqrecv.at[d],
            send_sem=y_send.at[d], recv_sem=y_recv.at[d],
            device_id={"mp": (y + d) % NY}, device_id_type=MESH,
        )

    barrier = pltpu.get_barrier_semaphore()
    for step in (1, -1, 3, -3):
        pl.semaphore_signal(barrier, inc=1, device_id=along_z(step), device_id_type=MESH)
    pl.semaphore_signal(barrier, inc=1, device_id={"span": sibling}, device_id_type=MESH)
    for d in (1, 2, 3):
        pl.semaphore_signal(barrier, inc=1, device_id={"span": (span + 2 * d) % 8}, device_id_type=MESH)
        pl.semaphore_signal(barrier, inc=1, device_id={"mp": (y + d) % NY}, device_id_type=MESH)
    pl.semaphore_wait(barrier, 11)

    z_copy(kv_ref, 3, 3).start()
    z_copy(kv_ref, 4, -3).start()
    z_copy(kv_ref, 1, 1).start()
    z_copy(kv_ref, 2, -1).start()
    c_copy(kv_ref, 0).start()
    for d in (1, 2, 3):
        @pl.when(x >= d)
        def _():
            q_copy(d).start()

    kvbuf[0, 0] = kv_ref[...]
    qbuf[0] = q_ref[...]
    acc[...] = jnp.zeros_like(acc)
    stat[...] = jnp.zeros_like(stat)
    stat[:, 0:1, :] = jnp.full((NX, 1, ROWS), LOW, jnp.float32)
    query_clips = NX - x
    key_position = lax.broadcasted_iota(jnp.int32, (TOK, 1), 0)

    def attend(which, base, moves, first_query):
        count = len(moves)
        keys = count * TOK
        clip = 2 * x + (core if which == 0 else 1 - core)
        length = tok_ref[clip]
        limits = [length - TOK * ((z - r + 2 * NZ) % NZ) for r in moves]
        values = kvbuf[which, pl.ds(base, count), 1].reshape(keys, HD)
        vtbuf[:, 0:keys] = values.T

        def one_query(i, carry):
            key_rows = kvbuf[which, pl.ds(base, count), 0].reshape(keys, HD)
            query_rows = jnp.concatenate(
                [qbuf[i, :, h * HD:(h + 1) * HD] for h in range(GROUP)], axis=0
            )
            scores = lax.dot_general(
                key_rows, query_rows, (((1,), (1,)), ((), ())),
                preferred_element_type=jnp.float32,
            )
            scores = jnp.concatenate(
                [
                    jnp.where(key_position < limits[n], scores[n * TOK:(n + 1) * TOK], -jnp.inf)
                    for n in range(count)
                ],
                axis=0,
            )
            old_max = stat[i, 0:1, :]
            new_max = jnp.maximum(old_max, jnp.max(scores, axis=0, keepdims=True))
            weights = jnp.exp2((scores - new_max) * EXP_SCALE)
            shrink = jnp.exp2((old_max - new_max) * EXP_SCALE)
            stat[i, 0:1, :] = new_max
            stat[i, 1:2, :] = stat[i, 1:2, :] * shrink + jnp.sum(weights, axis=0, keepdims=True)
            acc[i] = acc[i] * shrink + jnp.dot(
                vtbuf[:, 0:keys], weights.astype(jnp.bfloat16), preferred_element_type=jnp.float32
            )
            return carry

        lax.fori_loop(first_query, query_clips, one_query, 0)

    def forward(slot, dst_slot, step):
        z_copy(kvbuf.at[0, slot], dst_slot, step).start()

    def arrived(slot):
        z_copy(kvbuf.at[0, slot], slot, 1).wait_recv()

    def to_sibling(slot):
        c_copy(kvbuf.at[0, slot], slot).start()

    def from_sibling(slot):
        c_copy(kvbuf.at[0, slot], slot).wait_recv()

    def centres(k, last):
        right, left = 6 * k - 3, 6 * k - 2
        arrived(right)
        if last is None:
            forward(right, right + 6, 3)
        else:
            @pl.when(jnp.logical_not(last))
            def _():
                forward(right, right + 6, 3)
        forward(right, 6 * k - 1, -1)
        forward(right, 6 * k, 1)
        to_sibling(right)
        arrived(left)
        forward(left, 6 * k + 1, 1)
        if last is None:
            forward(left, left + 6, -3)
            forward(left, 6 * k + 2, -1)
        else:
            @pl.when(jnp.logical_not(last))
            def _():
                forward(left, left + 6, -3)
                forward(left, 6 * k + 2, -1)
        to_sibling(left)

    sib_first = jnp.where(core == 1, 0, 1)

    for slot in (1, 2):
        arrived(slot)
        to_sibling(slot)
    centres(1, None)
    for d in (1, 2, 3):
        @pl.when(x + d < NX)
        def _():
            q_copy(d).wait_recv()
    attend(0, 0, (0, 1, -1, 3, -3), 0)
    for slot in range(5):
        from_sibling(slot)
    attend(1, 0, (0, 1, -1, 3, -3), sib_first)

    def round_of(k, carry):
        base = 6 * k - 7
        for n in range(4):
            arrived(base + n)
            to_sibling(base + n)
        centres(k, k == 5)
        moves = (3 * k - 4, 3 * k - 2, 4 - 3 * k, 2 - 3 * k, 3 * k, -3 * k)
        attend(0, base, moves, 0)
        for n in range(6):
            from_sibling(base + n)
        attend(1, base, moves, sib_first)
        return carry

    lax.fori_loop(2, 6, round_of, 0)

    for slot in (29, 30, 31):
        arrived(slot)
        to_sibling(slot)
    attend(0, 29, (14, 16, -14), 0)
    for slot in (29, 30, 31):
        from_sibling(slot)
    attend(1, 29, (14, 16, -14), sib_first)

    for d in (1, 2, 3):
        @pl.when(x + d < NX)
        def _():
            obuf[d] = acc[d].astype(jnp.bfloat16)
            sbuf[d] = stat[d]
            o_copy(d).start()
            s_copy(d).start()

    own_level = noise_ref[span]
    level = lax.broadcasted_iota(jnp.int32, (gate_ref.shape[0], 1), 0)
    gate_row = jnp.sum(
        jnp.where(level == own_level, gate_ref[...].astype(jnp.float32), 0.0), axis=0, keepdims=True
    )
    scale_row = gain_ref[...].astype(jnp.float32) * (1.0 + gate_row)

    for d in (1, 2, 3):
        @pl.when(x >= d)
        def _():
            s_copy(d).wait_recv()
            o_copy(d).wait_recv()
            old_max, part_max = stat[0, 0:1, :], srecv[d, 0:1, :]
            new_max = jnp.maximum(old_max, part_max)
            mine = jnp.exp2((old_max - new_max) * EXP_SCALE)
            other = jnp.exp2((part_max - new_max) * EXP_SCALE)
            stat[0, 0:1, :] = new_max
            stat[0, 1:2, :] = stat[0, 1:2, :] * mine + srecv[d, 1:2, :] * other
            acc[0] = acc[0] * mine + orecv[d].astype(jnp.float32) * other

    attended = acc[0] / stat[0, 1:2, :]
    acc[0] = attended
    column = jnp.sum(attended * attended, axis=0, keepdims=True)
    pair = column[:, 0:128] + column[:, 128:256] + column[:, 256:384]
    square = jnp.broadcast_to(pair, (8, 128))
    square = square + pltpu.roll(square, TOK, 1)
    sqsend[...] = square
    for d in (1, 2, 3):
        y_copy(d).start()
    for d in (1, 2, 3):
        y_copy(d).wait_recv()
    total = square + sqrecv[1] + sqrecv[2] + sqrecv[3]
    inverse = lax.rsqrt(total[0:1, :] / (HEADS * HD) + 1e-06)
    token = z * TOK + lax.broadcasted_iota(jnp.int32, (TOK, 1), 0)
    usable = token < tok_ref[span]
    for p in range(GROUP // 2):
        turned = (acc[0, :, p * 128:(p + 1) * 128] * inverse).T
        for half in range(2):
            h = 2 * p + half
            piece = turned[half * TOK:(half + 1) * TOK] * scale_row[:, h * HD:(h + 1) * HD]
            out_ref[:, h * HD:(h + 1) * HD] = jnp.where(usable, piece, 0.0).astype(jnp.bfloat16)

    def drain(slot, carry):
        z_copy(kvbuf.at[0, slot], slot, 1).wait_send()
        return carry

    lax.fori_loop(1, NZ, drain, 0)

    def drain_sibling(slot, carry):
        c_copy(kvbuf.at[0, slot], slot).wait_send()
        return carry

    lax.fori_loop(0, NZ, drain_sibling, 0)
    for d in (1, 2, 3):
        y_copy(d).wait_send()

        @pl.when(x >= d)
        def _():
            q_copy(d).wait_send()

        @pl.when(x + d < NX)
        def _():
            o_copy(d).wait_send()
            s_copy(d).wait_send()


def per_device(queries, keys_values, clip_tokens, noise_level, level_gate, out_gain):
    vmem = pl.BlockSpec(memory_space=pltpu.VMEM)
    smem = pl.BlockSpec(memory_space=pltpu.SMEM)
    dma = pltpu.SemaphoreType.DMA
    out = pl.pallas_call(
        kernel,
        out_shape=jax.ShapeDtypeStruct((TOK, GROUP * HD), jnp.bfloat16),
        in_specs=[smem, smem, vmem, vmem, vmem, vmem],
        out_specs=vmem,
        scratch_shapes=[
            pltpu.VMEM((2, NZ, 2, TOK, HD), jnp.bfloat16),
            pltpu.VMEM((HD, 6 * TOK), jnp.bfloat16),
            pltpu.VMEM((NX, TOK, GROUP * HD), jnp.bfloat16),
            pltpu.VMEM((NX, HD, ROWS), jnp.float32),
            pltpu.VMEM((NX, 8, ROWS), jnp.float32),
            pltpu.VMEM((NX, HD, ROWS), jnp.bfloat16),
            pltpu.VMEM((NX, 8, ROWS), jnp.float32),
            pltpu.VMEM((NX, HD, ROWS), jnp.bfloat16),
            pltpu.VMEM((NX, 8, ROWS), jnp.float32),
            pltpu.VMEM((8, 128), jnp.float32),
            pltpu.VMEM((NY, 8, 128), jnp.float32),
            dma((NZ,)), dma((NZ,)), dma((NZ,)), dma((NZ,)),
            dma((NX,)), dma((NX,)), dma((NX,)), dma((NX,)),
            dma((NX,)), dma((NX,)), dma((NY,)), dma((NY,)),
        ],
        compiler_params=pltpu.CompilerParams(collective_id=0, has_side_effects=True),
        name="clip_attention",
    )(
        clip_tokens,
        noise_level,
        queries[0],
        keys_values[:, 0],
        level_gate,
        out_gain.reshape(1, GROUP * HD),
    )
    return out[None]


def solution(mesh):
    placed = (
        P("span", "seq", "mp"),
        P(None, "span", "seq", "mp"),
        P(),
        P(),
        P(None, "mp"),
        P("mp"),
    )
    return jax.shard_map(
        per_device, mesh=mesh, in_specs=placed, out_specs=P("span", "seq", "mp"), check_vma=False
    )
```

```python
import functools
import math

import jax
import jax.numpy as jnp
from jax import lax
from jax.experimental import pallas as pl
from jax.experimental.pallas import tpu as pltpu
from jax.sharding import PartitionSpec as P

HEADS = 24
KVH = 4
HD = 128
GROUP = HEADS // KVH
TOK = 64
NX = 4
NZ = 32
NY = 4
ROWS = GROUP * TOK
EXP_SCALE = math.log2(math.e) / math.sqrt(HD)
LOW = -1e30
MESH = pl.DeviceIdType.MESH


def kernel(
    tok_hbm, noise_hbm, q_hbm, kv_hbm, gate_hbm, gain_hbm, out_ref,
    tok_ref, noise_ref, gate_ref, gain_ref, in_sem,
    kvbuf, vtbuf, qbuf, acc, stat, obuf, sbuf, orecv, srecv, sqsend, sqrecv,
    z_send, z_recv, c_send, c_recv, q_send, q_recv, o_send, o_recv, s_send, s_recv, y_send, y_recv,
):
    span = lax.axis_index("span")
    z = lax.axis_index("seq")
    y = lax.axis_index("mp")
    x = span // 2
    core = span % 2
    sibling = span + 1 - 2 * core

    def along_z(step):
        return {"seq": (z + step + NZ) % NZ}

    def z_copy(src, dst_slot, step):
        return pltpu.make_async_remote_copy(
            src_ref=src, dst_ref=kvbuf.at[0, dst_slot],
            send_sem=z_send.at[dst_slot], recv_sem=z_recv.at[dst_slot],
            device_id=along_z(step), device_id_type=MESH,
        )

    def both_copy(src, dst_slot, step):
        return pltpu.make_async_remote_copy(
            src_ref=src, dst_ref=kvbuf.at[1, dst_slot],
            send_sem=c_send.at[dst_slot], recv_sem=c_recv.at[dst_slot],
            device_id={"span": sibling, "seq": (z + step + NZ) % NZ}, device_id_type=MESH,
        )

    def c_copy(src, slot):
        return pltpu.make_async_remote_copy(
            src_ref=src, dst_ref=kvbuf.at[1, slot],
            send_sem=c_send.at[slot], recv_sem=c_recv.at[slot],
            device_id={"span": sibling}, device_id_type=MESH,
        )

    def q_copy(d):
        return pltpu.make_async_remote_copy(
            src_ref=qbuf.at[0], dst_ref=qbuf.at[d],
            send_sem=q_send.at[d], recv_sem=q_recv.at[d],
            device_id={"span": (span - 2 * d + 8) % 8}, device_id_type=MESH,
        )

    def o_copy(d):
        return pltpu.make_async_remote_copy(
            src_ref=obuf.at[d], dst_ref=orecv.at[d],
            send_sem=o_send.at[d], recv_sem=o_recv.at[d],
            device_id={"span": (span + 2 * d) % 8}, device_id_type=MESH,
        )

    def s_copy(d):
        return pltpu.make_async_remote_copy(
            src_ref=sbuf.at[d], dst_ref=srecv.at[d],
            send_sem=s_send.at[d], recv_sem=s_recv.at[d],
            device_id={"span": (span + 2 * d) % 8}, device_id_type=MESH,
        )

    def y_copy(d):
        return pltpu.make_async_remote_copy(
            src_ref=sqsend, dst_ref=sqrecv.at[d],
            send_sem=y_send.at[d], recv_sem=y_recv.at[d],
            device_id={"mp": (y + d) % NY}, device_id_type=MESH,
        )

    loads = [
        pltpu.make_async_copy(src, dst, in_sem.at[n])
        for n, (src, dst) in enumerate(
            (
                (kv_hbm, kvbuf.at[0, 0]), (q_hbm, qbuf.at[0]), (gate_hbm, gate_ref),
                (gain_hbm, gain_ref), (tok_hbm, tok_ref), (noise_hbm, noise_ref),
            )
        )
    ]
    barrier = pltpu.get_barrier_semaphore()
    for load in loads:
        load.start()
    for step in (1, -1, 3, -3):
        pl.semaphore_signal(barrier, inc=1, device_id=along_z(step), device_id_type=MESH)
    pl.semaphore_signal(barrier, inc=1, device_id={"span": sibling}, device_id_type=MESH)
    for d in (1, 2, 3):
        pl.semaphore_signal(barrier, inc=1, device_id={"span": (span + 2 * d) % 8}, device_id_type=MESH)
        pl.semaphore_signal(barrier, inc=1, device_id={"mp": (y + d) % NY}, device_id_type=MESH)
    for step in (1, -1):
        pl.semaphore_signal(
            barrier, inc=1, device_id={"span": sibling, "seq": (z + step + NZ) % NZ}, device_id_type=MESH
        )
    acc[...] = jnp.zeros_like(acc)
    stat[...] = jnp.zeros_like(stat)
    stat[:, 0:1, :] = jnp.full((NX, 1, ROWS), LOW, jnp.float32)
    loads[0].wait()
    pl.semaphore_wait(barrier, 13)

    own = kvbuf.at[0, 0]
    z_copy(own, 3, 3).start()
    z_copy(own, 4, -3).start()
    z_copy(own, 1, 1).start()
    z_copy(own, 2, -1).start()
    c_copy(own, 0).start()
    loads[1].wait()
    loads[4].wait()
    for d in (1, 2, 3):
        @pl.when(x >= d)
        def _():
            q_copy(d).start()

    query_clips = NX - x
    key_position = lax.broadcasted_iota(jnp.int32, (TOK, 1), 0)

    def attend(which, base, moves, queries):
        count = len(moves)
        keys = count * TOK
        clip = 2 * x + (core if which == 0 else 1 - core)
        length = tok_ref[clip]
        limits = [length - TOK * ((z - r + 2 * NZ) % NZ) for r in moves]
        values = kvbuf[which, pl.ds(base, count), 1].reshape(keys, HD)
        vtbuf[which, :, 0:keys] = values.T

        def one_query(i):
            key_rows = kvbuf[which, pl.ds(base, count), 0].reshape(keys, HD)
            query_rows = jnp.concatenate(
                [qbuf[i, :, h * HD:(h + 1) * HD] for h in range(GROUP)], axis=0
            )
            scores = lax.dot_general(
                key_rows, query_rows, (((1,), (1,)), ((), ())),
                preferred_element_type=jnp.float32,
            )
            scores = jnp.concatenate(
                [
                    jnp.where(key_position < limits[n], scores[n * TOK:(n + 1) * TOK], -jnp.inf)
                    for n in range(count)
                ],
                axis=0,
            )
            old_max = stat[i, 0:1, :]
            new_max = jnp.maximum(old_max, jnp.max(scores, axis=0, keepdims=True))
            weights = jnp.exp2((scores - new_max) * EXP_SCALE)
            shrink = jnp.exp2((old_max - new_max) * EXP_SCALE)
            stat[i, 0:1, :] = new_max
            stat[i, 1:2, :] = stat[i, 1:2, :] * shrink + jnp.sum(weights, axis=0, keepdims=True)
            acc[i] = acc[i] * shrink + jnp.dot(
                vtbuf[which, :, 0:keys], weights.astype(jnp.bfloat16), preferred_element_type=jnp.float32
            )

        if queries is None:
            return one_query

        def step(i, carry):
            one_query(i)
            return carry

        lax.fori_loop(queries, query_clips, step, 0)

    def forward(slot, dst_slot, step):
        z_copy(kvbuf.at[0, slot], dst_slot, step).start()

    def forward_both(slot, dst_slot, step):
        forward(slot, dst_slot, step)
        both_copy(kvbuf.at[0, slot], dst_slot, step).start()

    def arrived(slot):
        z_copy(kvbuf.at[0, slot], slot, 1).wait_recv()

    def to_sibling(slot):
        c_copy(kvbuf.at[0, slot], slot).start()

    def from_sibling(slot):
        c_copy(kvbuf.at[0, slot], slot).wait_recv()

    def centres(k, last):
        right, left = 6 * k - 3, 6 * k - 2
        arrived(right)
        if last is None:
            forward(right, right + 6, 3)
            arrived(left)
            forward(left, left + 6, -3)
            forward(right, 6 * k, 1)
            forward(right, 6 * k - 1, -1)
            forward(left, 6 * k + 2, -1)
            forward(left, 6 * k + 1, 1)
        else:
            @pl.when(last)
            def _():
                forward_both(right, 6 * k, 1)
                forward_both(right, 6 * k - 1, -1)

            @pl.when(jnp.logical_not(last))
            def _():
                forward(right, right + 6, 3)

            arrived(left)

            @pl.when(last)
            def _():
                forward_both(left, 6 * k + 1, 1)

            @pl.when(jnp.logical_not(last))
            def _():
                forward(left, left + 6, -3)
                forward(right, 6 * k, 1)
                forward(right, 6 * k - 1, -1)
                forward(left, 6 * k + 2, -1)
                forward(left, 6 * k + 1, 1)

        to_sibling(right)
        to_sibling(left)

    def leaves(base):
        for n in range(4):
            arrived(base + n)
            to_sibling(base + n)

    def moves_of(k):
        return (3 * k - 4, 3 * k - 2, 4 - 3 * k, 2 - 3 * k, 3 * k, -3 * k)

    sib_first = jnp.where(core == 1, 0, 1)
    first_moves = (0, 1, -1, 3, -3)

    for slot in (1, 2):
        arrived(slot)
        to_sibling(slot)
    centres(1, None)
    for d in (1, 2, 3):
        @pl.when(x + d < NX)
        def _():
            q_copy(d).wait_recv()
    attend(0, 0, first_moves, 0)
    leaves(5)
    centres(2, None)
    for slot in range(5):
        from_sibling(slot)
    attend(1, 0, first_moves, sib_first)
    attend(0, 5, moves_of(2), 0)

    def round_of(k, carry):
        base = 6 * k - 7
        leaves(base)
        centres(k, k == 5)
        for n in range(6):
            from_sibling(base - 6 + n)
        attend(1, base - 6, moves_of(k - 1), sib_first)
        attend(0, base, moves_of(k), 0)
        return carry

    lax.fori_loop(3, 6, round_of, 0)
    for n in range(6):
        from_sibling(23 + n)
    attend(1, 23, moves_of(5), sib_first)

    for slot in (29, 30, 31):
        arrived(slot)
    mine = attend(0, 29, (14, 16, -14), None)
    for slot in (29, 30, 31):
        from_sibling(slot)
    other = attend(1, 29, (14, 16, -14), None)

    for d in (2, 3, 1):
        @pl.when(x + d < NX)
        def _():
            mine(d)
            other(d)
            obuf[d] = acc[d].astype(jnp.bfloat16)
            sbuf[d] = stat[d]
            o_copy(d).start()
            s_copy(d).start()
    mine(0)

    @pl.when(core == 1)
    def _():
        other(0)

    loads[2].wait()
    loads[3].wait()
    loads[5].wait()
    own_level = noise_ref[span]
    level = lax.broadcasted_iota(jnp.int32, (gate_ref.shape[0], 1), 0)
    gate_row = jnp.sum(
        jnp.where(level == own_level, gate_ref[...].astype(jnp.float32), 0.0), axis=0, keepdims=True
    )
    scale_row = gain_ref[...].astype(jnp.float32).reshape(1, GROUP * HD) * (1.0 + gate_row)

    for d in (1, 2, 3):
        @pl.when(x >= d)
        def _():
            s_copy(d).wait_recv()
            o_copy(d).wait_recv()
            old_max, part_max = stat[0, 0:1, :], srecv[d, 0:1, :]
            new_max = jnp.maximum(old_max, part_max)
            mine = jnp.exp2((old_max - new_max) * EXP_SCALE)
            other = jnp.exp2((part_max - new_max) * EXP_SCALE)
            stat[0, 0:1, :] = new_max
            stat[0, 1:2, :] = stat[0, 1:2, :] * mine + srecv[d, 1:2, :] * other
            acc[0] = acc[0] * mine + orecv[d].astype(jnp.float32) * other

    attended = acc[0] / stat[0, 1:2, :]
    acc[0] = attended
    column = jnp.sum(attended * attended, axis=0, keepdims=True)
    pair = column[:, 0:128] + column[:, 128:256] + column[:, 256:384]
    square = jnp.broadcast_to(pair, (8, 128))
    square = square + pltpu.roll(square, TOK, 1)
    sqsend[...] = square
    for d in (2, 1, 3):
        y_copy(d).start()
    for d in (1, 2, 3):
        y_copy(d).wait_recv()
    total = square + sqrecv[1] + sqrecv[2] + sqrecv[3]
    inverse = lax.rsqrt(total[0:1, :] / (HEADS * HD) + 1e-06)
    token = z * TOK + lax.broadcasted_iota(jnp.int32, (TOK, 1), 0)
    usable = token < tok_ref[span]
    for p in range(GROUP // 2):
        turned = (acc[0, :, p * 128:(p + 1) * 128] * inverse).T
        for half in range(2):
            h = 2 * p + half
            piece = turned[half * TOK:(half + 1) * TOK] * scale_row[:, h * HD:(h + 1) * HD]
            out_ref[:, h * HD:(h + 1) * HD] = jnp.where(usable, piece, 0.0).astype(jnp.bfloat16)

    def drain(slot, carry):
        z_copy(kvbuf.at[0, slot], slot, 1).wait_send()
        return carry

    lax.fori_loop(1, NZ, drain, 0)

    def drain_sibling(slot, carry):
        c_copy(kvbuf.at[0, slot], slot).wait_send()
        return carry

    lax.fori_loop(0, NZ, drain_sibling, 0)
    for d in (1, 2, 3):
        y_copy(d).wait_send()

        @pl.when(x >= d)
        def _():
            q_copy(d).wait_send()

        @pl.when(x + d < NX)
        def _():
            o_copy(d).wait_send()
            s_copy(d).wait_send()


def per_device(queries, keys_values, clip_tokens, noise_level, level_gate, out_gain):
    vmem = pl.BlockSpec(memory_space=pltpu.VMEM)
    hbm = pl.BlockSpec(memory_space=pltpu.HBM)
    dma = pltpu.SemaphoreType.DMA
    out = pl.pallas_call(
        kernel,
        out_shape=jax.ShapeDtypeStruct((TOK, GROUP * HD), jnp.bfloat16),
        in_specs=[hbm] * 6,
        out_specs=vmem,
        scratch_shapes=[
            pltpu.SMEM(clip_tokens.shape, jnp.int32),
            pltpu.SMEM(noise_level.shape, jnp.int32),
            pltpu.VMEM(level_gate.shape, jnp.bfloat16),
            pltpu.VMEM(out_gain.shape, jnp.bfloat16),
            dma((6,)),
            pltpu.VMEM((2, NZ, 2, TOK, HD), jnp.bfloat16),
            pltpu.VMEM((2, HD, 6 * TOK), jnp.bfloat16),
            pltpu.VMEM((NX, TOK, GROUP * HD), jnp.bfloat16),
            pltpu.VMEM((NX, HD, ROWS), jnp.float32),
            pltpu.VMEM((NX, 8, ROWS), jnp.float32),
            pltpu.VMEM((NX, HD, ROWS), jnp.bfloat16),
            pltpu.VMEM((NX, 8, ROWS), jnp.float32),
            pltpu.VMEM((NX, HD, ROWS), jnp.bfloat16),
            pltpu.VMEM((NX, 8, ROWS), jnp.float32),
            pltpu.VMEM((8, 128), jnp.float32),
            pltpu.VMEM((NY, 8, 128), jnp.float32),
            dma((NZ,)), dma((NZ,)), dma((NZ,)), dma((NZ,)),
            dma((NX,)), dma((NX,)), dma((NX,)), dma((NX,)),
            dma((NX,)), dma((NX,)), dma((NY,)), dma((NY,)),
        ],
        compiler_params=pltpu.CompilerParams(collective_id=0, has_side_effects=True, vmem_limit_bytes=32 * 2**20),
        name="clip_attention",
    )(
        *(
            pltpu.with_memory_space_constraint(a, pltpu.HBM)
            for a in (clip_tokens, noise_level, queries[0], keys_values[:, 0], level_gate, out_gain)
        ),
    )
    return out[None]


def solution(mesh):
    placed = (
        P("span", "seq", "mp"),
        P(None, "span", "seq", "mp"),
        P(),
        P(),
        P(None, "mp"),
        P("mp"),
    )
    return jax.shard_map(
        per_device, mesh=mesh, in_specs=placed, out_specs=P("span", "seq", "mp"), check_vma=False
    )
```

```python
import functools
import math

import jax
import jax.numpy as jnp
from jax import lax
from jax.experimental import pallas as pl
from jax.experimental.pallas import tpu as pltpu
from jax.sharding import PartitionSpec as P

HEADS = 24
KVH = 4
HD = 128
GROUP = HEADS // KVH
TOK = 64
NX = 4
NZ = 32
NY = 4
ROWS = GROUP * TOK
EXP_SCALE = math.log2(math.e) / math.sqrt(HD)
LOW = -1e30
MESH = pl.DeviceIdType.MESH


def kernel(
    tok_hbm, noise_hbm, q_hbm, kv_hbm, gate_hbm, gain_hbm, out_ref,
    tok_ref, noise_ref, gate_ref, gain_ref, in_sem,
    kvbuf, vtbuf, qbuf, acc, stat, obuf, sbuf, orecv, srecv, sqsend, sqrecv,
    z_send, z_recv, c_send, c_recv, q_send, q_recv, o_send, o_recv, s_send, s_recv, y_send, y_recv,
):
    span = lax.axis_index("span")
    z = lax.axis_index("seq")
    y = lax.axis_index("mp")
    x = span // 2
    core = span % 2
    sibling = span + 1 - 2 * core

    def along_z(step):
        return {"seq": (z + step + NZ) % NZ}

    def z_copy(src, dst_slot, step):
        return pltpu.make_async_remote_copy(
            src_ref=src, dst_ref=kvbuf.at[0, dst_slot],
            send_sem=z_send.at[dst_slot], recv_sem=z_recv.at[dst_slot],
            device_id=along_z(step), device_id_type=MESH,
        )

    def both_copy(src, dst_slot, step):
        return pltpu.make_async_remote_copy(
            src_ref=src, dst_ref=kvbuf.at[1, dst_slot],
            send_sem=c_send.at[dst_slot], recv_sem=c_recv.at[dst_slot],
            device_id={"span": sibling, "seq": (z + step + NZ) % NZ}, device_id_type=MESH,
        )

    def c_copy(src, slot):
        return pltpu.make_async_remote_copy(
            src_ref=src, dst_ref=kvbuf.at[1, slot],
            send_sem=c_send.at[slot], recv_sem=c_recv.at[slot],
            device_id={"span": sibling}, device_id_type=MESH,
        )

    def q_copy(d):
        return pltpu.make_async_remote_copy(
            src_ref=qbuf.at[0], dst_ref=qbuf.at[d],
            send_sem=q_send.at[d], recv_sem=q_recv.at[d],
            device_id={"span": (span - 2 * d + 8) % 8}, device_id_type=MESH,
        )

    def o_copy(d):
        return pltpu.make_async_remote_copy(
            src_ref=obuf.at[d], dst_ref=orecv.at[d],
            send_sem=o_send.at[d], recv_sem=o_recv.at[d],
            device_id={"span": (span + 2 * d) % 8}, device_id_type=MESH,
        )

    def s_copy(d):
        return pltpu.make_async_remote_copy(
            src_ref=sbuf.at[d], dst_ref=srecv.at[d],
            send_sem=s_send.at[d], recv_sem=s_recv.at[d],
            device_id={"span": (span + 2 * d) % 8}, device_id_type=MESH,
        )

    def y_copy(d):
        return pltpu.make_async_remote_copy(
            src_ref=sqsend, dst_ref=sqrecv.at[d],
            send_sem=y_send.at[d], recv_sem=y_recv.at[d],
            device_id={"mp": (y + d) % NY}, device_id_type=MESH,
        )

    loads = [
        pltpu.make_async_copy(src, dst, in_sem.at[n])
        for n, (src, dst) in enumerate(
            (
                (kv_hbm, kvbuf.at[0, 0]), (q_hbm, qbuf.at[0]), (gate_hbm, gate_ref),
                (gain_hbm, gain_ref), (tok_hbm, tok_ref), (noise_hbm, noise_ref),
            )
        )
    ]
    barrier = pltpu.get_barrier_semaphore()
    for load in loads:
        load.start()
    for step in (1, -1, 3, -3):
        pl.semaphore_signal(barrier, inc=1, device_id=along_z(step), device_id_type=MESH)
    pl.semaphore_signal(barrier, inc=1, device_id={"span": sibling}, device_id_type=MESH)
    for d in (1, 2, 3):
        pl.semaphore_signal(barrier, inc=1, device_id={"span": (span + 2 * d) % 8}, device_id_type=MESH)
        pl.semaphore_signal(barrier, inc=1, device_id={"mp": (y + d) % NY}, device_id_type=MESH)
    for step in (1, -1):
        pl.semaphore_signal(
            barrier, inc=1, device_id={"span": sibling, "seq": (z + step + NZ) % NZ}, device_id_type=MESH
        )
    acc[...] = jnp.zeros_like(acc)
    stat[...] = jnp.zeros_like(stat)
    stat[:, 0:1, :] = jnp.full((NX, 1, ROWS), LOW, jnp.float32)
    loads[0].wait()
    pl.semaphore_wait(barrier, 13)

    own = kvbuf.at[0, 0]
    z_copy(own, 3, 3).start()
    z_copy(own, 4, -3).start()
    z_copy(own, 1, 1).start()
    z_copy(own, 2, -1).start()
    c_copy(own, 0).start()
    loads[1].wait()
    loads[4].wait()
    for d in (1, 2, 3):
        @pl.when(x >= d)
        def _():
            q_copy(d).start()

    query_clips = NX - x
    key_position = lax.broadcasted_iota(jnp.int32, (TOK, 1), 0)

    def attend(parts, queries):
        keys = sum(len(moves) for _, _, moves in parts) * TOK

        def rows_of(kind):
            return jnp.concatenate(
                [kvbuf[which, pl.ds(base, len(moves)), kind].reshape(-1, HD) for which, base, moves in parts],
                axis=0,
            )

        vtbuf[:, 0:keys] = rows_of(1).T
        limits = []
        for which, _, moves in parts:
            length = tok_ref[2 * x + (core if which == 0 else 1 - core)]
            limits += [(which, length - TOK * ((z - r + 2 * NZ) % NZ)) for r in moves]

        def one_query(i):
            later_clip = (i == 0) & (core == 0)
            query_rows = jnp.concatenate(
                [qbuf[i, :, h * HD:(h + 1) * HD] for h in range(GROUP)], axis=0
            )
            scores = lax.dot_general(
                rows_of(0), query_rows, (((1,), (1,)), ((), ())),
                preferred_element_type=jnp.float32,
            )
            scores = jnp.concatenate(
                [
                    jnp.where(
                        key_position < (jnp.where(later_clip, 0, limit) if which else limit),
                        scores[n * TOK:(n + 1) * TOK],
                        -jnp.inf,
                    )
                    for n, (which, limit) in enumerate(limits)
                ],
                axis=0,
            )
            old_max = stat[i, 0:1, :]
            new_max = jnp.maximum(old_max, jnp.max(scores, axis=0, keepdims=True))
            weights = jnp.exp2((scores - new_max) * EXP_SCALE)
            shrink = jnp.exp2((old_max - new_max) * EXP_SCALE)
            stat[i, 0:1, :] = new_max
            stat[i, 1:2, :] = stat[i, 1:2, :] * shrink + jnp.sum(weights, axis=0, keepdims=True)
            acc[i] = acc[i] * shrink + jnp.dot(
                vtbuf[:, 0:keys], weights.astype(jnp.bfloat16), preferred_element_type=jnp.float32
            )

        if queries is None:
            return one_query

        def step(i, carry):
            one_query(i)
            return carry

        lax.fori_loop(queries, query_clips, step, 0)

    def forward(slot, dst_slot, step):
        z_copy(kvbuf.at[0, slot], dst_slot, step).start()

    def forward_both(slot, dst_slot, step):
        forward(slot, dst_slot, step)
        both_copy(kvbuf.at[0, slot], dst_slot, step).start()

    def arrived(slot):
        z_copy(kvbuf.at[0, slot], slot, 1).wait_recv()

    def to_sibling(slot):
        c_copy(kvbuf.at[0, slot], slot).start()

    def from_sibling(slot):
        c_copy(kvbuf.at[0, slot], slot).wait_recv()

    def centres(k, last):
        right, left = 6 * k - 3, 6 * k - 2
        arrived(right)
        if last:
            forward_both(right, 6 * k, 1)
            forward_both(right, 6 * k - 1, -1)
            arrived(left)
            forward_both(left, 6 * k + 1, 1)
        else:
            forward(right, right + 6, 3)
            arrived(left)
            forward(left, left + 6, -3)
            forward(right, 6 * k, 1)
            forward(right, 6 * k - 1, -1)
            forward(left, 6 * k + 2, -1)
            forward(left, 6 * k + 1, 1)
        to_sibling(right)
        to_sibling(left)

    def leaves(base):
        for n in range(4):
            arrived(base + n)
            to_sibling(base + n)

    def moves_of(k):
        return (3 * k - 4, 3 * k - 2, 4 - 3 * k, 2 - 3 * k, 3 * k, -3 * k)

    first_moves = (0, 1, -1, 3, -3)
    last_moves = (14, 16, -14)

    centres(1, False)
    for slot in (1, 2):
        arrived(slot)
        to_sibling(slot)
    for d in (1, 2, 3):
        @pl.when(x + d < NX)
        def _():
            q_copy(d).wait_recv()
    attend(((0, 0, first_moves),), 0)
    centres(2, False)
    leaves(5)
    for slot in range(5):
        from_sibling(slot)
    attend(((1, 0, first_moves), (0, 5, moves_of(2))), 0)

    def round_of(k, carry):
        base = 6 * k - 7
        centres(k, False)
        leaves(base)
        for n in range(6):
            from_sibling(base - 6 + n)
        attend(((1, base - 6, moves_of(k - 1)), (0, base, moves_of(k))), 0)
        return carry

    lax.fori_loop(3, 5, round_of, 0)
    centres(5, True)
    leaves(23)
    for n in range(6):
        from_sibling(17 + n)
    attend(((1, 17, moves_of(4)), (0, 23, moves_of(5))), 0)

    for slot in (29, 30, 31):
        arrived(slot)
    for slot in range(23, 32):
        from_sibling(slot)
    late = attend(((1, 23, moves_of(5)), (0, 29, last_moves), (1, 29, last_moves)), None)

    for d in (2, 1, 3):
        @pl.when(x + d < NX)
        def _():
            late(d)
            obuf[d] = acc[d].astype(jnp.bfloat16)
            sbuf[d] = stat[d]
            o_copy(d).start()
            s_copy(d).start()
    late(0)

    loads[2].wait()
    loads[3].wait()
    loads[5].wait()
    own_level = noise_ref[span]
    level = lax.broadcasted_iota(jnp.int32, (gate_ref.shape[0], 1), 0)
    gate_row = jnp.sum(
        jnp.where(level == own_level, gate_ref[...].astype(jnp.float32), 0.0), axis=0, keepdims=True
    )
    scale_row = gain_ref[...].astype(jnp.float32).reshape(1, GROUP * HD) * (1.0 + gate_row)

    for d in (1, 2, 3):
        @pl.when(x >= d)
        def _():
            s_copy(d).wait_recv()
            o_copy(d).wait_recv()
            old_max, part_max = stat[0, 0:1, :], srecv[d, 0:1, :]
            new_max = jnp.maximum(old_max, part_max)
            mine = jnp.exp2((old_max - new_max) * EXP_SCALE)
            other = jnp.exp2((part_max - new_max) * EXP_SCALE)
            stat[0, 0:1, :] = new_max
            stat[0, 1:2, :] = stat[0, 1:2, :] * mine + srecv[d, 1:2, :] * other
            acc[0] = acc[0] * mine + orecv[d].astype(jnp.float32) * other

    attended = acc[0] / stat[0, 1:2, :]
    acc[0] = attended
    column = jnp.sum(attended * attended, axis=0, keepdims=True)
    pair = column[:, 0:128] + column[:, 128:256] + column[:, 256:384]
    square = jnp.broadcast_to(pair, (8, 128))
    square = square + pltpu.roll(square, TOK, 1)
    sqsend[...] = square
    for d in (2, 1, 3):
        y_copy(d).start()
    for d in (1, 2, 3):
        y_copy(d).wait_recv()
    total = square + sqrecv[1] + sqrecv[2] + sqrecv[3]
    inverse = lax.rsqrt(total[0:1, :] / (HEADS * HD) + 1e-06)
    token = z * TOK + lax.broadcasted_iota(jnp.int32, (TOK, 1), 0)
    usable = token < tok_ref[span]
    for p in range(GROUP // 2):
        turned = (acc[0, :, p * 128:(p + 1) * 128] * inverse).T
        for half in range(2):
            h = 2 * p + half
            piece = turned[half * TOK:(half + 1) * TOK] * scale_row[:, h * HD:(h + 1) * HD]
            out_ref[:, h * HD:(h + 1) * HD] = jnp.where(usable, piece, 0.0).astype(jnp.bfloat16)

    def drain(slot, carry):
        z_copy(kvbuf.at[0, slot], slot, 1).wait_send()
        return carry

    lax.fori_loop(1, NZ, drain, 0)

    def drain_sibling(slot, carry):
        c_copy(kvbuf.at[0, slot], slot).wait_send()
        return carry

    lax.fori_loop(0, NZ, drain_sibling, 0)
    for d in (1, 2, 3):
        y_copy(d).wait_send()

        @pl.when(x >= d)
        def _():
            q_copy(d).wait_send()

        @pl.when(x + d < NX)
        def _():
            o_copy(d).wait_send()
            s_copy(d).wait_send()


def per_device(queries, keys_values, clip_tokens, noise_level, level_gate, out_gain):
    vmem = pl.BlockSpec(memory_space=pltpu.VMEM)
    hbm = pl.BlockSpec(memory_space=pltpu.HBM)
    dma = pltpu.SemaphoreType.DMA
    out = pl.pallas_call(
        kernel,
        out_shape=jax.ShapeDtypeStruct((TOK, GROUP * HD), jnp.bfloat16),
        in_specs=[hbm] * 6,
        out_specs=vmem,
        scratch_shapes=[
            pltpu.SMEM(clip_tokens.shape, jnp.int32),
            pltpu.SMEM(noise_level.shape, jnp.int32),
            pltpu.VMEM(level_gate.shape, jnp.bfloat16),
            pltpu.VMEM(out_gain.shape, jnp.bfloat16),
            dma((6,)),
            pltpu.VMEM((2, NZ, 2, TOK, HD), jnp.bfloat16),
            pltpu.VMEM((HD, 12 * TOK), jnp.bfloat16),
            pltpu.VMEM((NX, TOK, GROUP * HD), jnp.bfloat16),
            pltpu.VMEM((NX, HD, ROWS), jnp.float32),
            pltpu.VMEM((NX, 8, ROWS), jnp.float32),
            pltpu.VMEM((NX, HD, ROWS), jnp.bfloat16),
            pltpu.VMEM((NX, 8, ROWS), jnp.float32),
            pltpu.VMEM((NX, HD, ROWS), jnp.bfloat16),
            pltpu.VMEM((NX, 8, ROWS), jnp.float32),
            pltpu.VMEM((8, 128), jnp.float32),
            pltpu.VMEM((NY, 8, 128), jnp.float32),
            dma((NZ,)), dma((NZ,)), dma((NZ,)), dma((NZ,)),
            dma((NX,)), dma((NX,)), dma((NX,)), dma((NX,)),
            dma((NX,)), dma((NX,)), dma((NY,)), dma((NY,)),
        ],
        compiler_params=pltpu.CompilerParams(collective_id=0, has_side_effects=True, vmem_limit_bytes=32 * 2**20),
        name="clip_attention",
    )(
        *(
            pltpu.with_memory_space_constraint(a, pltpu.HBM)
            for a in (clip_tokens, noise_level, queries[0], keys_values[:, 0], level_gate, out_gain)
        ),
    )
    return out[None]


def solution(mesh):
    placed = (
        P("span", "seq", "mp"),
        P(None, "span", "seq", "mp"),
        P(),
        P(),
        P(None, "mp"),
        P("mp"),
    )
    return jax.shard_map(
        per_device, mesh=mesh, in_specs=placed, out_specs=P("span", "seq", "mp"), check_vma=False
    )
```
